768 devices in a mesh: row: 8 (over y_hi, x), col: 96 (over z, y_lo, core).
Axes of the slice: x: 4, y: 8 (y_hi: 2, y_lo: 4; y = y_hi * 4 + y_lo), z: 12, core: 2. Of those that a mesh axis runs over, the one named last changes fastest.
Arguments:
- tokens: bfloat16 [384, 8192], P('col', 'row'), may hold values from -6 to 6
- out_grad: bfloat16 [384, 8192], P('col', 'row'), may hold values from -6 to 6
- gate_weight: bfloat16 [8192, 27648], P('row', 'col'), may hold values from -0.0625 to 0.0625
- up_weight: bfloat16 [8192, 27648], P('row', 'col'), may hold values from -0.0625 to 0.0625
- down_weight: bfloat16 [27648, 8192], P('col', 'row'), may hold values from -0.0390625 to 0.0390625
Outputs:
- tokens_grad: bfloat16 [384, 8192], P('col', 'row')
- gate_grad: bfloat16 [8192, 27648], P('row', 'col')
- up_grad: bfloat16 [8192, 27648], P('row', 'col')
- down_grad: bfloat16 [27648, 8192], P('col', 'row')
The draws below stay inside these ranges and needn't reach their ends.
All inputs are finite; a program needn't handle non-finite values.
Results may differ from the reference program's by a relative error of at most 0.0049.
Values may be sent and summed in bfloat16 or wider, within the bound.
No kernel may reach another device: no remote copies, remote signals or barrier semaphores. Data moves between devices by JAX's collectives and lax.ppermute only.
A program may use at most 32 MiB of HBM per device.

```python
import jax
import jax.numpy as jnp

D = 8192
FF = 27648
TOKENS = 384


def levels(rng, shape, shards, least, largest):
    def one(axis_at, shards_of):
        draws = jax.random.uniform(jax.random.fold_in(jax.random.fold_in(rng, 6), axis_at), (shards_of,), jnp.float32, least / len(shards), largest / len(shards))
        return jnp.repeat(jnp.exp(draws), shape[axis_at] // shards_of).reshape((-1,) + (1,) * (len(shape) - axis_at - 1))

    factor_of = one(*shards[0])
    for cut in shards[1:]:
        factor_of = factor_of * one(*cut)
    return factor_of


def noise(key, extent, scale, most, shards=(), kind=jnp.bfloat16):
    loudness = levels(key, extent, shards, -0.22, 0.18) if shards else 1.0
    entries = jax.random.normal(key, extent, jnp.float32) * scale * loudness
    return jnp.minimum(jnp.maximum(entries, -most), most).astype(kind)


def setup_inputs(seed: int = 0) -> dict:
    key_of = jax.random.split(jax.random.key(seed), 6)
    tokens = noise(key_of[0], (TOKENS, D), 1.0, 6.0, ((0, 96), (1, 8)))
    out_grad = noise(key_of[1], (TOKENS, D), 1.0, 6.0, ((0, 96), (1, 8)))
    gate_weight = noise(key_of[2], (D, FF), D ** -0.5, 0.0625, ((0, 8), (1, 96)))
    up_weight = noise(key_of[3], (D, FF), D ** -0.5, 0.0625, ((0, 8), (1, 96)))
    down_weight = noise(key_of[4], (FF, D), FF ** -0.5, 0.0390625, ((0, 96), (1, 8)))
    return {"tokens": tokens, "out_grad": out_grad, "gate_weight": gate_weight, "up_weight": up_weight, "down_weight": down_weight}


def reference(tokens, out_grad, gate_weight, up_weight, down_weight):
    factor = float(TOKENS) ** -0.5
    gate_pre = jnp.dot(tokens, gate_weight, preferred_element_type=jnp.float32)
    up_pre = jnp.dot(tokens, up_weight, preferred_element_type=jnp.float32)
    hidden_grad = jnp.dot(out_grad, down_weight.T, preferred_element_type=jnp.float32)
    sig = jax.nn.sigmoid(gate_pre)
    act = gate_pre * sig
    hidden = (act * up_pre).astype(jnp.bfloat16)
    up_delta = (hidden_grad * act).astype(jnp.bfloat16)
    gate_delta = (hidden_grad * up_pre * sig * (1.0 + gate_pre * (1.0 - sig))).astype(jnp.bfloat16)
    down_grad = (jnp.dot(hidden.T, out_grad, preferred_element_type=jnp.float32) * factor).astype(jnp.bfloat16)
    gate_grad = (jnp.dot(tokens.T, gate_delta, preferred_element_type=jnp.float32) * factor).astype(jnp.bfloat16)
    up_grad = (jnp.dot(tokens.T, up_delta, preferred_element_type=jnp.float32) * factor).astype(jnp.bfloat16)
    tokens_grad = (jnp.dot(gate_delta, gate_weight.T, preferred_element_type=jnp.float32)
                   + jnp.dot(up_delta, up_weight.T, preferred_element_type=jnp.float32)).astype(jnp.bfloat16)
    return tokens_grad, gate_grad, up_grad, down_grad
```

```python
import jax
import jax.numpy as jnp
import numpy as np
from jax import lax
from jax.sharding import Mesh, PartitionSpec as P

F32 = jnp.float32
BF16 = jnp.bfloat16
SWAP = [(0, 1), (1, 0)]
ROW = ("yh", "x")
CHIPS = ("z", "yl")


def dot(left, right, left_dim, right_dim):
    return lax.dot_general(
        left, right, (((left_dim,), (right_dim,)), ((), ())), preferred_element_type=F32
    )


def pointwise(gate_pre, up_pre, hidden_grad):
    sig = jax.nn.sigmoid(gate_pre)
    act = gate_pre * sig
    hidden = (act * up_pre).astype(BF16)
    up_delta = (hidden_grad * act).astype(BF16)
    gate_delta = (hidden_grad * up_pre * sig * (1.0 + gate_pre * (1.0 - sig))).astype(BF16)
    return hidden, gate_delta, up_delta


def exchange_sum(parts, axes):
    me = lax.axis_index(axes)
    own = lax.dynamic_index_in_dim(parts, me, 0)
    got = lax.all_to_all(parts.astype(BF16), axes, 0, 0).astype(F32)
    at = lax.broadcasted_iota(jnp.int32, got.shape, 0)
    return jnp.sum(jnp.where(at == me, own, got), axis=0)


def gather(block, axes):
    copies = jnp.broadcast_to(block[None], (lax.axis_size(axes),) + block.shape)
    return lax.all_to_all(copies, axes, 0, 0)


def per_device(tokens, out_grad, gate_weight, up_weight, down_weight):
    rows, width = tokens.shape
    units = gate_weight.shape[1]
    n_row = lax.axis_size(ROW)
    mine = gather(jnp.concatenate([tokens, out_grad], 1), CHIPS)
    mine = mine.reshape(-1, 2 * width)
    panel = jnp.concatenate([mine, lax.ppermute(mine, "core", SWAP)])
    panel_in, panel_grad = panel[:, :width], panel[:, width:]
    count = panel.shape[0]
    factor = float(count) ** (-0.5)

    share = units // n_row
    pre = jnp.concatenate(
        [
            dot(gate_weight, panel_in, 0, 1).reshape(n_row, share, count),
            dot(up_weight, panel_in, 0, 1).reshape(n_row, share, count),
            dot(down_weight, panel_grad, 1, 1).reshape(n_row, share, count),
        ],
        axis=1,
    )
    total = exchange_sum(pre, ROW)
    deltas = pointwise(total[:share], total[share : 2 * share], total[2 * share :])
    deltas = gather(jnp.concatenate(deltas), ROW)
    hidden = deltas[:, :share].reshape(units, count)
    gate_delta = deltas[:, share : 2 * share].reshape(units, count)
    up_delta = deltas[:, 2 * share :].reshape(units, count)

    partial = dot(gate_delta, gate_weight, 0, 1) + dot(up_delta, up_weight, 0, 1)
    half = count // 2
    acc = partial[:half] + lax.ppermute(partial[half:], "core", SWAP)
    tokens_grad = exchange_sum(acc.reshape(-1, rows, width), CHIPS).astype(BF16)

    down_grad = (dot(hidden, panel_grad, 1, 0) * factor).astype(BF16)
    gate_grad = (dot(panel_in, gate_delta, 0, 1) * factor).astype(BF16)
    up_grad = (dot(panel_in, up_delta, 0, 1) * factor).astype(BF16)
    return tokens_grad, gate_grad, up_grad, down_grad


def solution(mesh):
    n_row, n_col = mesh.devices.shape
    grid = np.asarray(mesh.devices).reshape(2, n_row // 2, n_col // 8, 4, 2)
    fine = Mesh(grid, ("yh", "x", "z", "yl", "core"))
    row, col = ("yh", "x"), ("z", "yl", "core")
    return jax.shard_map(
        per_device,
        mesh=fine,
        in_specs=(P(col, row), P(col, row), P(row, col), P(row, col), P(col, row)),
        out_specs=(P(col, row), P(row, col), P(row, col), P(col, row)),
        check_vma=False,
    )
```

```python
import jax
import jax.numpy as jnp
import numpy as np
from jax import lax
from jax.sharding import Mesh, PartitionSpec as P

F32 = jnp.float32
BF16 = jnp.bfloat16
SWAP = [(0, 1), (1, 0)]
CHIPS = ("yl", "z")


def dot(left, right, left_dim, right_dim):
    return lax.dot_general(
        left, right, (((left_dim,), (right_dim,)), ((), ())), preferred_element_type=F32
    )


def pointwise(gate_pre, up_pre, hidden_grad):
    sig = jax.nn.sigmoid(gate_pre)
    act = gate_pre * sig
    hidden = (act * up_pre).astype(BF16)
    up_delta = (hidden_grad * act).astype(BF16)
    gate_delta = (hidden_grad * up_pre * sig * (1.0 + gate_pre * (1.0 - sig))).astype(BF16)
    return hidden, gate_delta, up_delta


def exchange_sum(parts, axes):
    me = lax.axis_index(axes)
    own = lax.dynamic_index_in_dim(parts, me, 0)
    got = lax.all_to_all(parts.astype(BF16), axes, 0, 0).astype(F32)
    at = lax.broadcasted_iota(jnp.int32, got.shape, 0)
    return jnp.sum(jnp.where(at == me, own, got), axis=0)


def gather(block, axes):
    copies = jnp.broadcast_to(block[None], (lax.axis_size(axes),) + block.shape)
    return lax.all_to_all(copies, axes, 0, 0)


def per_device(tokens, out_grad, gate_weight, up_weight, down_weight):
    rows, width = tokens.shape
    units = gate_weight.shape[1]
    n_x = lax.axis_size("x")
    mine = lax.all_gather(jnp.concatenate([tokens, out_grad], 1), "z", axis=0)
    mine = lax.all_gather(mine, "yl", axis=0)
    mine = mine.reshape(-1, 2 * width)
    panel = jnp.concatenate([mine, lax.ppermute(mine, "core", SWAP)])
    panel_in, panel_grad = panel[:, :width], panel[:, width:]
    count = panel.shape[0]
    factor = float(count) ** (-0.5)

    share = units // n_x
    pre = jnp.stack(
        [
            dot(gate_weight, panel_in, 0, 1).reshape(n_x, share, count),
            dot(up_weight, panel_in, 0, 1).reshape(n_x, share, count),
            dot(down_weight, panel_grad, 1, 1).reshape(n_x, share, count),
        ],
        axis=1,
    )
    part = exchange_sum(pre, "x")
    total = part + lax.ppermute(part.astype(BF16), "yh", SWAP).astype(F32)
    deltas = gather(jnp.stack(pointwise(total[0], total[1], total[2])), "x")
    hidden = deltas[:, 0].reshape(units, count)
    gate_delta = deltas[:, 1].reshape(units, count)
    up_delta = deltas[:, 2].reshape(units, count)

    partial = dot(gate_delta, gate_weight, 0, 1) + dot(up_delta, up_weight, 0, 1)
    half = count // 2
    acc = partial[:half] + lax.ppermute(partial[half:], "core", SWAP)
    tokens_grad = exchange_sum(acc.reshape(-1, rows, width), CHIPS).astype(BF16)

    down_grad = (dot(hidden, panel_grad, 1, 0) * factor).astype(BF16)
    gate_grad = (dot(panel_in, gate_delta, 0, 1) * factor).astype(BF16)
    up_grad = (dot(panel_in, up_delta, 0, 1) * factor).astype(BF16)
    return tokens_grad, gate_grad, up_grad, down_grad


def solution(mesh):
    n_row, n_col = mesh.devices.shape
    grid = np.asarray(mesh.devices).reshape(2, n_row // 2, n_col // 8, 4, 2)
    fine = Mesh(grid, ("yh", "x", "z", "yl", "core"))
    row, col = ("yh", "x"), ("z", "yl", "core")
    return jax.shard_map(
        per_device,
        mesh=fine,
        in_specs=(P(col, row), P(col, row), P(row, col), P(row, col), P(col, row)),
        out_specs=(P(col, row), P(row, col), P(row, col), P(col, row)),
        check_vma=False,
    )
```

```python
import jax
import jax.numpy as jnp
import numpy as np
from jax import lax
from jax.sharding import Mesh, PartitionSpec as P

F32 = jnp.float32
BF16 = jnp.bfloat16
SWAP = [(0, 1), (1, 0)]
CHIPS = ("yl", "z")


def dot(left, right, left_dim, right_dim):
    return lax.dot_general(
        left, right, (((left_dim,), (right_dim,)), ((), ())), preferred_element_type=F32
    )


def pointwise(gate_pre, up_pre, hidden_grad):
    sig = jax.nn.sigmoid(gate_pre)
    act = gate_pre * sig
    hidden = (act * up_pre).astype(BF16)
    up_delta = (hidden_grad * act).astype(BF16)
    gate_delta = (hidden_grad * up_pre * sig * (1.0 + gate_pre * (1.0 - sig))).astype(BF16)
    return hidden, gate_delta, up_delta


def exchange_sum(parts, axes):
    me, n = lax.axis_index(axes), lax.axis_size(axes)
    rows = parts.shape[0] // n
    own = lax.dynamic_slice_in_dim(parts, me * rows, rows, 0)[None]
    sent = parts.astype(BF16).reshape((n, rows) + parts.shape[1:])
    got = lax.all_to_all(sent, axes, 0, 0).astype(F32)
    at = lax.broadcasted_iota(jnp.int32, got.shape, 0)
    return jnp.sum(jnp.where(at == me, own, got), axis=0)


def gather(block, axes):
    copies = jnp.broadcast_to(block[None], (lax.axis_size(axes),) + block.shape)
    return lax.all_to_all(copies, axes, 0, 0)


def per_device(tokens, out_grad, gate_weight, up_weight, down_weight):
    rows, width = tokens.shape
    units = gate_weight.shape[1]
    n_x = lax.axis_size("x")
    mine = gather(jnp.concatenate([tokens, out_grad], 1), "z")
    mine = lax.all_gather(mine, "yl", axis=0)
    mine = mine.reshape(-1, 2 * width)
    panel = jnp.concatenate([mine, lax.ppermute(mine, "core", SWAP)])
    panel_in, panel_grad = panel[:, :width], panel[:, width:]
    count = panel.shape[0]
    factor = float(count) ** (-0.5)

    share = units // n_x
    pre = jnp.stack(
        [
            dot(gate_weight, panel_in, 0, 1).reshape(n_x, share, count),
            dot(up_weight, panel_in, 0, 1).reshape(n_x, share, count),
            dot(down_weight, panel_grad, 1, 1).reshape(n_x, share, count),
        ],
        axis=1,
    )
    part = exchange_sum(pre, "x")[0]
    total = part + lax.ppermute(part.astype(BF16), "yh", SWAP).astype(F32)
    deltas = gather(jnp.stack(pointwise(total[0], total[1], total[2])), "x")
    hidden = deltas[:, 0].reshape(units, count)
    gate_delta = deltas[:, 1].reshape(units, count)
    up_delta = deltas[:, 2].reshape(units, count)

    partial = dot(gate_delta, gate_weight, 0, 1) + dot(up_delta, up_weight, 0, 1)
    half = count // 2
    acc = partial[:half] + lax.ppermute(partial[half:], "core", SWAP)
    acc = lax.optimization_barrier(acc.astype(BF16)).reshape(-1, rows, width)
    acc = lax.all_to_all(acc, CHIPS, 0, 0)
    tokens_grad = jnp.sum(acc.astype(F32), axis=0).astype(BF16)

    down_grad = (dot(hidden, panel_grad, 1, 0) * factor).astype(BF16)
    gate_grad = (dot(panel_in, gate_delta, 0, 1) * factor).astype(BF16)
    up_grad = (dot(panel_in, up_delta, 0, 1) * factor).astype(BF16)
    return tokens_grad, gate_grad, up_grad, down_grad


def solution(mesh):
    n_row, n_col = mesh.devices.shape
    grid = np.asarray(mesh.devices).reshape(2, n_row // 2, n_col // 8, 4, 2)
    fine = Mesh(grid, ("yh", "x", "z", "yl", "core"))
    row, col = ("yh", "x"), ("z", "yl", "core")
    return jax.shard_map(
        per_device,
        mesh=fine,
        in_specs=(P(col, row), P(col, row), P(row, col), P(row, col), P(col, row)),
        out_specs=(P(col, row), P(row, col), P(row, col), P(col, row)),
        check_vma=False,
    )
```

```python
import jax
import jax.numpy as jnp
import numpy as np
from jax import lax
from jax.sharding import Mesh, PartitionSpec as P

F32 = jnp.float32
BF16 = jnp.bfloat16
SWAP = [(0, 1), (1, 0)]
CHIPS = ("yl", "z")


def dot(left, right, left_dim, right_dim):
    return lax.dot_general(
        left, right, (((left_dim,), (right_dim,)), ((), ())), preferred_element_type=F32
    )


def pointwise(gate_pre, up_pre, hidden_grad):
    sig = jax.nn.sigmoid(gate_pre)
    act = gate_pre * sig
    hidden = (act * up_pre).astype(BF16)
    up_delta = (hidden_grad * act).astype(BF16)
    gate_delta = (hidden_grad * up_pre * sig * (1.0 + gate_pre * (1.0 - sig))).astype(BF16)
    return hidden, gate_delta, up_delta


def exchange_sum(parts, axes):
    me = lax.axis_index(axes)
    own = lax.dynamic_index_in_dim(parts, me, 0)
    sent, own = lax.optimization_barrier((parts.astype(BF16), own))
    got = lax.all_to_all(sent, axes, 0, 0).astype(F32)
    at = lax.broadcasted_iota(jnp.int32, got.shape, 0)
    return jnp.sum(jnp.where(at == me, own, got), axis=0)


def gather(block, axes):
    copies = jnp.broadcast_to(block[None], (lax.axis_size(axes),) + block.shape)
    return lax.all_to_all(copies, axes, 0, 0)


def per_device(tokens, out_grad, gate_weight, up_weight, down_weight):
    rows, width = tokens.shape
    units = gate_weight.shape[1]
    n_x = lax.axis_size("x")
    mine = gather(jnp.concatenate([tokens, out_grad], 1), "z")
    mine = lax.all_gather(mine, "yl", axis=0)
    mine = mine.reshape(-1, 2 * width)
    panel = jnp.concatenate([mine, lax.ppermute(mine, "core", SWAP)])
    panel_in, panel_grad = panel[:, :width], panel[:, width:]
    count = panel.shape[0]
    factor = float(count) ** (-0.5)

    share = units // n_x
    pre = jnp.stack(
        [
            dot(gate_weight, panel_in, 0, 1).reshape(n_x, share, count),
            dot(up_weight, panel_in, 0, 1).reshape(n_x, share, count),
            dot(down_weight, panel_grad, 1, 1).reshape(n_x, share, count),
        ],
        axis=1,
    )
    part = exchange_sum(pre, "x")
    total = part + lax.ppermute(part.astype(BF16), "yh", SWAP).astype(F32)
    deltas = gather(jnp.stack(pointwise(total[0], total[1], total[2])), "x")
    hidden = deltas[:, 0].reshape(units, count)
    gate_delta = deltas[:, 1].reshape(units, count)
    up_delta = deltas[:, 2].reshape(units, count)

    partial = dot(gate_delta, gate_weight, 0, 1) + dot(up_delta, up_weight, 0, 1)
    half = count // 2
    got = lax.ppermute(partial[half:], "core", SWAP)
    up_grad = (dot(panel_in, up_delta, 0, 1) * factor).astype(BF16)
    acc = (partial[:half] + got).astype(BF16)
    acc, up_grad = lax.optimization_barrier((acc, up_grad))
    acc = lax.all_to_all(acc.reshape(-1, rows, width), CHIPS, 0, 0)
    tokens_grad = jnp.sum(acc.astype(F32), axis=0).astype(BF16)
    tokens_grad, hidden, gate_delta = lax.optimization_barrier((tokens_grad, hidden, gate_delta))
    down_grad = (dot(hidden, panel_grad, 1, 0) * factor).astype(BF16)
    gate_grad = (dot(panel_in, gate_delta, 0, 1) * factor).astype(BF16)
    return tokens_grad, gate_grad, up_grad, down_grad


def solution(mesh):
    n_row, n_col = mesh.devices.shape
    grid = np.asarray(mesh.devices).reshape(2, n_row // 2, n_col // 8, 4, 2)
    fine = Mesh(grid, ("yh", "x", "z", "yl", "core"))
    row, col = ("yh", "x"), ("z", "yl", "core")
    return jax.shard_map(
        per_device,
        mesh=fine,
        in_specs=(P(col, row), P(col, row), P(row, col), P(row, col), P(col, row)),
        out_specs=(P(col, row), P(row, col), P(row, col), P(col, row)),
        check_vma=False,
    )
```

```python
import jax
import jax.numpy as jnp
import numpy as np
from jax import lax
from jax.sharding import Mesh, PartitionSpec as P

F32 = jnp.float32
BF16 = jnp.bfloat16
SWAP = [(0, 1), (1, 0)]
CHIPS = ("yl", "z")


def dot(left, right, left_dim, right_dim):
    return lax.dot_general(
        left, right, (((left_dim,), (right_dim,)), ((), ())), preferred_element_type=F32
    )


def pointwise(gate_pre, up_pre, hidden_grad):
    sig = jax.nn.sigmoid(gate_pre)
    act = gate_pre * sig
    hidden = (act * up_pre).astype(BF16)
    up_delta = (hidden_grad * act).astype(BF16)
    gate_delta = (hidden_grad * up_pre * sig * (1.0 + gate_pre * (1.0 - sig))).astype(BF16)
    return hidden, gate_delta, up_delta


def exchange_sum(parts, axes):
    me = lax.axis_index(axes)
    own = lax.dynamic_index_in_dim(parts, me, 0)
    mask = lax.broadcasted_iota(jnp.int32, (parts.shape[0],) + (1,) * (parts.ndim - 1), 0) == me
    sent, own, mask = lax.optimization_barrier((parts.astype(BF16), own, mask))
    got = lax.all_to_all(sent, axes, 0, 0).astype(F32)
    return jnp.sum(jnp.where(mask, own, got), axis=0)


def gather(block, axes):
    copies = jnp.broadcast_to(block[None], (lax.axis_size(axes),) + block.shape)
    return lax.all_to_all(copies, axes, 0, 0)


def per_device(tokens, out_grad, gate_weight, up_weight, down_weight):
    rows, width = tokens.shape
    units = gate_weight.shape[1]
    n_x = lax.axis_size("x")
    mine = gather(jnp.concatenate([tokens, out_grad], 1), "z")
    mine = lax.all_gather(mine, "yl", axis=0)
    mine = mine.reshape(-1, 2 * width)
    panel = jnp.concatenate([mine, lax.ppermute(mine, "core", SWAP)])
    panel_in, panel_grad = panel[:, :width], panel[:, width:]
    count = panel.shape[0]
    factor = float(count) ** (-0.5)

    share = units // n_x
    pre = jnp.stack(
        [
            dot(gate_weight, panel_in, 0, 1).reshape(n_x, share, count),
            dot(up_weight, panel_in, 0, 1).reshape(n_x, share, count),
            dot(down_weight, panel_grad, 1, 1).reshape(n_x, share, count),
        ],
        axis=1,
    )
    part = exchange_sum(pre, "x")
    total = part + lax.ppermute(part.astype(BF16), "yh", SWAP).astype(F32)
    deltas = gather(jnp.stack(pointwise(total[0], total[1], total[2])), "x")
    hidden = deltas[:, 0].reshape(units, count)
    gate_delta = deltas[:, 1].reshape(units, count)
    up_delta = deltas[:, 2].reshape(units, count)

    partial = dot(gate_delta, gate_weight, 0, 1) + dot(up_delta, up_weight, 0, 1)
    half = count // 2
    got = lax.ppermute(partial[half:], "core", SWAP)
    up_grad = (dot(panel_in, up_delta, 0, 1) * factor).astype(BF16)
    acc = (partial[:half] + got).astype(BF16)
    acc, up_grad = lax.optimization_barrier((acc, up_grad))
    acc = lax.all_to_all(acc.reshape(-1, rows, width), CHIPS, 0, 0)
    tokens_grad = jnp.sum(acc.astype(F32), axis=0).astype(BF16)
    down_grad = (dot(hidden, panel_grad, 1, 0) * factor).astype(BF16)
    gate_grad = (dot(panel_in, gate_delta, 0, 1) * factor).astype(BF16)
    return tokens_grad, gate_grad, up_grad, down_grad


def solution(mesh):
    n_row, n_col = mesh.devices.shape
    grid = np.asarray(mesh.devices).reshape(2, n_row // 2, n_col // 8, 4, 2)
    fine = Mesh(grid, ("yh", "x", "z", "yl", "core"))
    row, col = ("yh", "x"), ("z", "yl", "core")
    return jax.shard_map(
        per_device,
        mesh=fine,
        in_specs=(P(col, row), P(col, row), P(row, col), P(row, col), P(col, row)),
        out_specs=(P(col, row), P(row, col), P(row, col), P(col, row)),
        check_vma=False,
    )
```

```python
import jax
import jax.numpy as jnp
import numpy as np
from jax import lax
from jax.sharding import Mesh, PartitionSpec as P

F32 = jnp.float32
BF16 = jnp.bfloat16
SWAP = [(0, 1), (1, 0)]
CHIPS = ("z", "yl")


def dot(left, right, left_dim, right_dim):
    return lax.dot_general(
        left, right, (((left_dim,), (right_dim,)), ((), ())), preferred_element_type=F32
    )


def pointwise(gate_pre, up_pre, hidden_grad):
    sig = jax.nn.sigmoid(gate_pre)
    act = gate_pre * sig
    hidden = (act * up_pre).astype(BF16)
    up_delta = (hidden_grad * act).astype(BF16)
    gate_delta = (hidden_grad * up_pre * sig * (1.0 + gate_pre * (1.0 - sig))).astype(BF16)
    return hidden, gate_delta, up_delta


def exchange_sum(parts, axes):
    me = lax.axis_index(axes)
    own = lax.dynamic_index_in_dim(parts, me, 0)
    mask = lax.broadcasted_iota(jnp.int32, (parts.shape[0],) + (1,) * (parts.ndim - 1), 0) == me
    sent, own, mask = lax.optimization_barrier((parts.astype(BF16), own, mask))
    got = lax.all_to_all(sent, axes, 0, 0).astype(F32)
    return jnp.sum(jnp.where(mask, own, got), axis=0)


def gather(block, axes):
    copies = jnp.broadcast_to(block[None], (lax.axis_size(axes),) + block.shape)
    return lax.all_to_all(copies, axes, 0, 0)


def per_device(tokens, out_grad, gate_weight, up_weight, down_weight):
    rows, width = tokens.shape
    units = gate_weight.shape[1]
    n_x = lax.axis_size("x")
    mine = gather(jnp.concatenate([tokens, out_grad], 1), "yl")
    mine = lax.all_gather(mine, "z", axis=0)
    mine = mine.reshape(-1, 2 * width)
    panel = jnp.concatenate([mine, lax.ppermute(mine, "core", SWAP)])
    panel_in, panel_grad = panel[:, :width], panel[:, width:]
    count = panel.shape[0]
    factor = float(count) ** (-0.5)

    share = units // n_x
    pre = jnp.stack(
        [
            dot(gate_weight, panel_in, 0, 1).reshape(n_x, share, count),
            dot(up_weight, panel_in, 0, 1).reshape(n_x, share, count),
            dot(down_weight, panel_grad, 1, 1).reshape(n_x, share, count),
        ],
        axis=1,
    )
    part = exchange_sum(pre, "x")
    total = part + lax.ppermute(part.astype(BF16), "yh", SWAP).astype(F32)
    deltas = gather(jnp.stack(pointwise(total[0], total[1], total[2])), "x")
    hidden = deltas[:, 0].reshape(units, count)
    gate_delta = deltas[:, 1].reshape(units, count)
    up_delta = deltas[:, 2].reshape(units, count)

    partial = dot(gate_delta, gate_weight, 0, 1) + dot(up_delta, up_weight, 0, 1)
    half = count // 2
    got = lax.ppermute(partial[half:], "core", SWAP)
    up_grad = (dot(panel_in, up_delta, 0, 1) * factor).astype(BF16)
    acc = (partial[:half] + got).astype(BF16)
    acc, up_grad = lax.optimization_barrier((acc, up_grad))
    acc = lax.all_to_all(acc.reshape(-1, rows, width), CHIPS, 0, 0)
    tokens_grad = jnp.sum(acc.astype(F32), axis=0).astype(BF16)
    down_grad = (dot(hidden, panel_grad, 1, 0) * factor).astype(BF16)
    gate_grad = (dot(panel_in, gate_delta, 0, 1) * factor).astype(BF16)
    return tokens_grad, gate_grad, up_grad, down_grad


def solution(mesh):
    n_row, n_col = mesh.devices.shape
    grid = np.asarray(mesh.devices).reshape(2, n_row // 2, n_col // 8, 4, 2)
    fine = Mesh(grid, ("yh", "x", "z", "yl", "core"))
    row, col = ("yh", "x"), ("z", "yl", "core")
    return jax.shard_map(
        per_device,
        mesh=fine,
        in_specs=(P(col, row), P(col, row), P(row, col), P(row, col), P(col, row)),
        out_specs=(P(col, row), P(row, col), P(row, col), P(col, row)),
        check_vma=False,
    )
```

```python
import jax
import jax.numpy as jnp
import numpy as np
from jax import lax
from jax.sharding import Mesh, PartitionSpec as P

F32 = jnp.float32
BF16 = jnp.bfloat16
SWAP = [(0, 1), (1, 0)]
CHIPS = ("z", "yl")


def dot(left, right, left_dim, right_dim):
    return lax.dot_general(
        left, right, (((left_dim,), (right_dim,)), ((), ())), preferred_element_type=F32
    )


def pointwise(gate_pre, up_pre, hidden_grad):
    sig = jax.nn.sigmoid(gate_pre)
    act = gate_pre * sig
    hidden = (act * up_pre).astype(BF16)
    up_delta = (hidden_grad * act).astype(BF16)
    gate_delta = (hidden_grad * up_pre * sig * (1.0 + gate_pre * (1.0 - sig))).astype(BF16)
    return hidden, gate_delta, up_delta


def exchange_sum(parts, axes):
    me = lax.axis_index(axes)
    own = lax.dynamic_index_in_dim(parts, me, 0)
    mask = lax.broadcasted_iota(jnp.int32, (parts.shape[0],) + (1,) * (parts.ndim - 1), 0) == me
    sent, own, mask = lax.optimization_barrier((parts.astype(BF16), own, mask))
    got = lax.all_to_all(sent, axes, 0, 0).astype(F32)
    return jnp.sum(jnp.where(mask, own, got), axis=0)


def gather(block, axes):
    copies = jnp.broadcast_to(block[None], (lax.axis_size(axes),) + block.shape)
    return lax.all_to_all(copies, axes, 0, 0)


def per_device(tokens, out_grad, gate_weight, up_weight, down_weight):
    rows, width = tokens.shape
    units = gate_weight.shape[1]
    n_x = lax.axis_size("x")
    mine = gather(jnp.concatenate([tokens, out_grad], 1), "yl")
    mine = lax.all_gather(mine, "z", axis=0)
    mine = mine.reshape(-1, 2 * width)
    panel = jnp.concatenate([mine, lax.ppermute(mine, "core", SWAP)])
    panel_in, panel_grad = panel[:, :width], panel[:, width:]
    count = panel.shape[0]
    factor = float(count) ** (-0.5)

    share = units // n_x
    pre = jnp.stack(
        [
            dot(gate_weight, panel_in, 0, 1).reshape(n_x, share, count),
            dot(up_weight, panel_in, 0, 1).reshape(n_x, share, count),
            dot(down_weight, panel_grad, 1, 1).reshape(n_x, share, count),
        ],
        axis=1,
    )
    part = exchange_sum(pre, "x")
    total = part + lax.ppermute(part.astype(BF16), "yh", SWAP).astype(F32)
    deltas = gather(jnp.stack(pointwise(total[0], total[1], total[2])), "x")
    hidden = deltas[:, 0].reshape(units, count)
    gate_delta = deltas[:, 1].reshape(units, count)
    up_delta = deltas[:, 2].reshape(units, count)

    half = count // 2
    give = dot(gate_delta[:, half:], gate_weight, 0, 1) + dot(up_delta[:, half:], up_weight, 0, 1)
    got = lax.ppermute(give, "core", SWAP)
    keep = lax.optimization_barrier(
        dot(gate_delta[:, :half], gate_weight, 0, 1) + dot(up_delta[:, :half], up_weight, 0, 1)
    )
    acc = lax.optimization_barrier((keep + got).astype(BF16))
    acc = lax.all_to_all(acc.reshape(-1, rows, width), CHIPS, 0, 0)
    tokens_grad = jnp.sum(acc.astype(F32), axis=0).astype(BF16)

    up_grad = (dot(panel_in, up_delta, 0, 1) * factor).astype(BF16)
    down_grad = (dot(hidden, panel_grad, 1, 0) * factor).astype(BF16)
    gate_grad = (dot(panel_in, gate_delta, 0, 1) * factor).astype(BF16)
    return tokens_grad, gate_grad, up_grad, down_grad


def solution(mesh):
    n_row, n_col = mesh.devices.shape
    grid = np.asarray(mesh.devices).reshape(2, n_row // 2, n_col // 8, 4, 2)
    fine = Mesh(grid, ("yh", "x", "z", "yl", "core"))
    row, col = ("yh", "x"), ("z", "yl", "core")
    return jax.shard_map(
        per_device,
        mesh=fine,
        in_specs=(P(col, row), P(col, row), P(row, col), P(row, col), P(col, row)),
        out_specs=(P(col, row), P(row, col), P(row, col), P(col, row)),
        check_vma=False,
    )
```
